32 devices in a mesh: pts: 8 (over y, x, core), val: 4 (over z).
Axes of the slice: x: 2, y: 2, z: 4, core: 2. Of those that a mesh axis runs over, the one named last changes fastest.
Arguments:
- trials: bfloat16 [2, 1024, 1024], P(None, 'val', 'pts'), may hold values from -6 to 6
- psi_val: bfloat16 [8192, 1024], P('pts', 'val'), may hold values from -0.1875 to 0.1875
- psi_cond: bfloat16 [8192, 1024], P('pts'), may hold values from -0.1875 to 0.1875
- kernel: bfloat16 [8192, 8192], P(None, ('pts', 'val')), may hold values from -0.5 to 0.5
- eps_val: float32 [1024], P('val'), may hold values from -1.75 to -0.25
- eps_cond: float32 [1024], replicated, may hold values from 0.5 to 1.5
Outputs:
- first: float32 [2, 1024, 1024], P(None, 'val', 'pts')
- filtered: float32 [2, 1024, 1024], P(None, 'val', 'pts')
The draws below stay inside these ranges and needn't reach their ends.
All inputs are finite; a program needn't handle non-finite values.
Results may differ from the reference program's by a relative error of at most 0.025.
Values may be sent and summed in bfloat16 or wider, within the bound.
A program may use at most 64 MiB of HBM per device.

```python
import jax
import jax.numpy as jnp
from jax import lax

NV = 1024
NC = 1024
NMU = 8192
K = 2
N_PTS = 8


def with_spikes(array, rng, source, target, blocks, factor):
    def block_of(position):
        return (jnp.arange(array.shape[position]) // (array.shape[position] // blocks)).reshape((-1,) + (1,) * (array.ndim - 1 - position))

    one_side = jax.random.permutation(rng, blocks)[block_of(target)]
    other_side = (block_of(target) + blocks // 2) % blocks
    return jnp.where((block_of(source) == one_side) | (block_of(source) == other_side), factor * array, array)


def steps_of(key, extent, shards, low, top_value):
    level = 1.0
    for dim, parts in shards:
        heights = jax.random.uniform(jax.random.fold_in(jax.random.fold_in(key, 6), dim), (parts,), jnp.float32, low / len(shards), top_value / len(shards))
        level = level * jnp.repeat(jnp.exp(heights), extent[dim] // parts).reshape((-1,) + (1,) * (len(extent) - 1 - dim))
    return level


def normal_values(stream_key, shape, width, limit, cuts=(), dtype=jnp.bfloat16):
    loudness = steps_of(stream_key, shape, cuts, -0.22, 0.18) if cuts else 1.0
    values = jax.random.normal(stream_key, shape, jnp.float32) * width * loudness
    return jnp.minimum(jnp.maximum(values, -limit), limit).astype(dtype)


def heavy_noise(stream_key, shape, scale, reach, split, heavy, held_as=jnp.bfloat16):
    drawn = scale * jax.random.normal(stream_key, shape, jnp.float32)
    if split:
        drawn = drawn * steps_of(stream_key, shape, split, -0.22, 0.18)
    return jnp.clip(with_spikes(drawn, jax.random.fold_in(stream_key, 3), *heavy), -reach, reach).astype(held_as)


def setup_inputs(seed: int = 0) -> dict:
    streams_of = jax.random.split(jax.random.key(seed), 7)
    return {
        "trials": normal_values(streams_of[0], (K, NV, NC), 1.0, 6.0, ((1, 4), (2, 8))),
        "psi_val": normal_values(streams_of[1], (NMU, NV), NV ** -0.5, 0.1875, ((0, 8), (1, 4))),
        "psi_cond": normal_values(streams_of[2], (NMU, NC), NC ** -0.5, 0.1875, ((0, 8),)),
        "kernel": heavy_noise(streams_of[3], (NMU, NMU), (NMU // 16) ** -0.5, 0.5, ((1, 32),), (1, 0, 32, 2.75)),
        "eps_val": jnp.clip(-1.75 + 1.5 * jax.random.uniform(streams_of[4], (NV,), jnp.float32) ** steps_of(streams_of[4], (NV,), ((0, 4),), -0.2, 0.2), -1.75, -0.25),
        "eps_cond": jnp.clip(jax.random.uniform(streams_of[5], (NC,), jnp.float32, 0.5, 1.5), 0.5, 1.5),
    }


center_shift = 1.75
half_width = 1.25


def apply_kernel(trial, psi_val, psi_cond, kernel):
    block_pts = NMU // N_PTS
    val_blocks = psi_val.reshape(N_PTS, block_pts, NV)
    cond_blocks = psi_cond.reshape(N_PTS, block_pts, NC)
    trial_wide = trial.astype(jnp.float32)

    def density(pieces):
        val_piece, cond_piece = pieces
        inner = jnp.einsum('kvc,mc->kvm', trial_wide, cond_piece.astype(jnp.float32))
        return jnp.einsum('mv,kvm->km', val_piece.astype(jnp.float32), inner)

    rho_blocks = lax.map(density, (val_blocks, cond_blocks))
    rho = jnp.transpose(rho_blocks, (1, 0, 2)).reshape(K, NMU).astype(jnp.bfloat16)
    image = jnp.einsum('km,nm->kn', rho.astype(jnp.float32), kernel.astype(jnp.float32))
    image_blocks = jnp.transpose(image.reshape(K, N_PTS, block_pts), (1, 0, 2))

    def accumulate(total, pieces):
        val_piece, cond_piece, image_piece = pieces
        weighted = (jnp.transpose(val_piece.astype(jnp.float32))[None] * image_piece[:, None, :]).astype(jnp.bfloat16)
        partial_sum = jnp.einsum('kvm,mc->kvc', weighted.astype(jnp.float32), cond_piece.astype(jnp.float32))
        rounded = lax.optimization_barrier(partial_sum.astype(jnp.bfloat16))
        return total + rounded.astype(jnp.float32), None

    start = jnp.zeros((K, NV, NC), jnp.float32)
    result, unused = lax.scan(accumulate, start, (val_blocks, cond_blocks, image_blocks))
    return result


def reference(trials, psi_val, psi_cond, kernel, eps_val, eps_cond):
    diff = (eps_cond[None, :] - eps_val[:, None] - center_shift)[None]
    first_image = apply_kernel(trials, psi_val, psi_cond, kernel)
    first = (diff * trials.astype(jnp.float32) + 2.0 * first_image) / half_width
    second_trial = first.astype(jnp.bfloat16)
    second_image = apply_kernel(second_trial, psi_val, psi_cond, kernel)
    filtered = 2.0 * (diff * second_trial.astype(jnp.float32) + 2.0 * second_image) / half_width - trials.astype(jnp.float32)
    return first, filtered
```

```python
import jax
import jax.numpy as jnp
from jax import lax
from jax.experimental import pallas as pl
from jax.experimental.pallas import tpu as pltpu
from jax.sharding import PartitionSpec as P

center_shift = 1.75
half_width = 1.25


def gathered_inner(local_trial, psi_cond):
    return jnp.einsum(
        "kvc,mc->kvm",
        lax.all_gather(local_trial, "pts", axis=2, tiled=True),
        psi_cond,
        preferred_element_type=jnp.float32,
    )


def orbital_terms(inner, psi_val, psi_cond, kernel):
    rho_part = jnp.einsum("mv,kvm->km", psi_val.astype(jnp.float32), inner)
    rho = lax.psum_scatter(rho_part, "val", scatter_dimension=1, tiled=True).astype(jnp.bfloat16)
    image_part = jnp.einsum("km,nm->kn", rho, kernel, preferred_element_type=jnp.float32)
    image_rows = lax.psum_scatter(
        image_part.astype(jnp.bfloat16), "pts", scatter_dimension=1, tiled=True
    ).astype(jnp.float32)
    image = lax.psum(image_rows, "val")
    weighted = (jnp.transpose(psi_val.astype(jnp.float32))[None] * image[:, None, :]).astype(
        jnp.bfloat16
    )
    return jnp.einsum("kvm,mc->kvc", weighted, psi_cond, preferred_element_type=jnp.float32)


def reduced(partial_sum):
    return lax.psum_scatter(
        partial_sum.astype(jnp.bfloat16), "pts", scatter_dimension=2, tiled=True
    ).astype(jnp.float32)


def local(trials, psi_val, psi_cond, kernel, eps_val, eps_cond):
    cols_own = trials.shape[2]
    index_pts = lax.axis_index("pts")
    diff_whole = (eps_cond[None, :] - eps_val[:, None] - center_shift)[None]
    diff_own = lax.dynamic_slice_in_dim(diff_whole, index_pts * cols_own, cols_own, 2)
    first_image = reduced(
        orbital_terms(gathered_inner(trials, psi_cond), psi_val, psi_cond, kernel)
    )
    first = (diff_own * trials.astype(jnp.float32) + 2.0 * first_image) / half_width
    second_trial = first.astype(jnp.bfloat16)
    second_inner = gathered_inner(second_trial, psi_cond)
    second_image = reduced(orbital_terms(second_inner, psi_val, psi_cond, kernel))
    filtered = 2.0 * (
        diff_own * second_trial.astype(jnp.float32) + 2.0 * second_image
    ) / half_width - trials.astype(jnp.float32)
    return (first, filtered)


F32, BF16 = jnp.float32, jnp.bfloat16
SWAP = (0, 2, 1, 3)
NT = (((1,), (1,)), ((), ()))


def fused_kernel(n_pts, n_val, x_ref, pv_hbm, pc_hbm, kern_hbm, ev_ref, ec_ref, first_ref, filt_ref,
                 pv, pvt, cond, kern, diff, second, xg, rs, rr, im, ir, ws, wr,
                 acc, part_out, part_in, link_out, link_in, load_sem, send_sem, recv_sem):
    p = lax.axis_index("pts")
    z = lax.axis_index("val")
    core = lax.rem(p, 2)
    n_k, rows, cols = x_ref.shape
    pts_own = pv.shape[0]
    width = rr.shape[3]

    def flipped(q, bit):
        return q + bit - 2 * bit * lax.rem(lax.div(q, bit), 2)

    bit_a, bit_b = 2 + 2 * core, 4 - 2 * core
    mate, nbr_a, nbr_b = flipped(p, 1), flipped(p, bit_a), flipped(p, bit_b)
    places = (p, nbr_a, nbr_b, flipped(nbr_a, bit_b))

    loads = [pltpu.make_async_copy(pv_hbm, pv, load_sem.at[0])]
    for j in range(4):
        for h in range(2):
            owner = places[j] if h == 0 else flipped(places[j], 1)
            at = pl.multiple_of(owner * cols, cols)
            loads.append(pltpu.make_async_copy(
                pc_hbm.at[:, pl.ds(at, cols)], cond.at[j, :, pl.ds(h * cols, cols)], load_sem.at[1 + 2 * j + h]))
    loads.append(pltpu.make_async_copy(kern_hbm, kern, load_sem.at[9]))
    for load in loads:
        load.start()

    barrier = pltpu.get_barrier_semaphore()
    for r in range(1, n_pts):
        pl.semaphore_signal(barrier, inc=1, device_id=(lax.rem(p + r, n_pts), z), device_id_type=pl.DeviceIdType.MESH)
    for s in range(1, n_val):
        pl.semaphore_signal(barrier, inc=1, device_id=(p, lax.rem(z + s, n_val)), device_id_type=pl.DeviceIdType.MESH)
    pl.semaphore_wait(barrier, n_pts + n_val - 2)

    sent = []

    def remote(it, n, src, dst, to_p, to_z):
        copy = pltpu.make_async_remote_copy(
            src_ref=src, dst_ref=dst, send_sem=send_sem.at[it, n], recv_sem=recv_sem.at[it, n],
            device_id=(to_p, to_z), device_id_type=pl.DeviceIdType.MESH)
        copy.start()
        sent.append(copy)
        return copy

    def gather_start(it, x):
        g = {}
        for k in range(n_k):
            g["a", k] = remote(it, k, x.at[k], xg.at[it, 1, 0, k], nbr_a, z)
            g["b", k] = remote(it, 2 + k, x.at[k], xg.at[it, 2, 0, k], nbr_b, z)
            g["m0", k] = remote(it, 4 + k, x.at[k], xg.at[it, 0, 1, k], mate, z)
        return g

    def density(it, j, x, rho):
        wide = cond.shape[1]
        step = 256
        left = x[...] if j == 0 else xg[it, j, 0]
        block = jnp.concatenate([left.reshape(n_k * rows, cols), xg[it, j, 1].reshape(n_k * rows, cols)], axis=1)
        out = []
        for t in range(wide // step):
            zz = lax.dot_general(block, cond[j, t * step:(t + 1) * step, :], NT, preferred_element_type=F32)
            scale = pvt[:, t * step:(t + 1) * step]
            for k in range(n_k):
                y = zz[k * rows:(k + 1) * rows] * scale
                out.append(jnp.sum(y.reshape(rows // 8, 8, step), axis=0))
        return out if rho is None else [u + w for u, w in zip(rho, out)]

    def apply(it, x):
        g = gather_start(it, x)
        if it == 0:
            loads[0].wait()
            pvt[...] = jnp.transpose(pv[...].astype(F32))
            diff[...] = (ec_ref[:, pl.ds(pl.multiple_of(p * cols, cols), cols)]
                         - jnp.transpose(jnp.broadcast_to(ev_ref[...], (cols, rows))) - center_shift)
            for load in loads[1:9]:
                load.wait()
        for k in range(n_k):
            g["a", k].wait_recv()
            g["d", k] = remote(it, 6 + k, xg.at[it, 1, 0, k], xg.at[it, 3, 0, k], nbr_b, z)
            g["m2", k] = remote(it, 8 + k, xg.at[it, 1, 0, k], xg.at[it, 2, 1, k], mate, z)
            g["b", k].wait_recv()
            g["m1", k] = remote(it, 10 + k, xg.at[it, 2, 0, k], xg.at[it, 1, 1, k], mate, z)
        for k in range(n_k):
            g["m0", k].wait_recv()
        rho = density(it, 0, x, None)
        for k in range(n_k):
            g["m1", k].wait_recv()
        rho = density(it, 1, x, rho)
        for k in range(n_k):
            g["d", k].wait_recv()
            g["m3", k] = remote(it, 12 + k, xg.at[it, 3, 0, k], xg.at[it, 3, 1, k], mate, z)
        for k in range(n_k):
            g["m2", k].wait_recv()
        rho = density(it, 2, x, rho)
        for k in range(n_k):
            g["m3", k].wait_recv()
        rho = density(it, 3, x, rho)

        summed = [jnp.sum(u, axis=0, keepdims=True) for u in rho]
        rho_part = jnp.concatenate(
            [jnp.concatenate(summed[k::n_k], axis=1) for k in range(n_k)], axis=0)
        for s in range(n_val):
            rs[it, s] = rho_part[:, s * width:(s + 1) * width]
        got = []
        for s in range(1, n_val):
            to = lax.rem(z + s, n_val)
            got.append(remote(it, 13 + s, rs.at[it, to], rr.at[it, s], p, to))
        own = rs[it, z]
        for s in range(1, n_val):
            got[s - 1].wait_recv()
            own = own + rr[it, s]
        own = own.astype(BF16)

        if it == 0:
            loads[9].wait()
        for t in range(n_pts):
            im[it, t] = lax.dot_general(own, kern[t * pts_own:(t + 1) * pts_own, :], NT, preferred_element_type=F32)
        got = []
        for r in range(1, n_pts):
            to = lax.rem(p + r, n_pts)
            got.append(remote(it, 16 + r, im.at[it, to], ir.at[it, r], to, z))
        total = im[it, p]
        for r in range(1, n_pts):
            got[r - 1].wait_recv()
            total = total + ir[it, r]
        ws[it] = total
        got = [remote(it, 23 + s, ws.at[it], wr.at[it, s], p, lax.rem(z + s, n_val)) for s in range(1, n_val)]
        for s in range(1, n_val):
            got[s - 1].wait_recv()
            total = total + wr[it, s]

        weighted = [(pvt[...] * total[k:k + 1]).astype(BF16) for k in range(n_k)]
        mated, relayed, from_a, from_b = {}, {}, {}, {}
        result = [None] * n_k

        def finish(j, k):
            mated[j, k].wait_recv()
            value = acc[j, k] + part_in[it, j, k].astype(F32)
            if j == 3:
                link_out[it, 0, k] = value.astype(BF16)
                relayed[k] = remote(it, 35 + k, link_out.at[it, 0, k], link_in.at[it, 0, k], nbr_b, z)
            elif j == 2:
                link_out[it, 2, k] = value.astype(BF16)
                from_b[k] = remote(it, 37 + k, link_out.at[it, 2, k], link_in.at[it, 2, k], nbr_b, z)
            elif j == 1:
                relayed[k].wait_recv()
                link_out[it, 1, k] = (value + link_in[it, 0, k].astype(F32)).astype(BF16)
                from_a[k] = remote(it, 39 + k, link_out.at[it, 1, k], link_in.at[it, 1, k], nbr_a, z)
            else:
                from_b[k].wait_recv()
                value = value + link_in[it, 2, k].astype(F32)
                from_a[k].wait_recv()
                result[k] = value + link_in[it, 1, k].astype(F32)

        order = [(j, k) for j in (3, 2, 1, 0) for k in range(n_k)]
        for n, (j, k) in enumerate(order):
            both = jnp.dot(weighted[k], cond[j], preferred_element_type=F32)
            acc[j, k] = both[:, :cols]
            part_out[it, j, k] = both[:, cols:].astype(BF16)
            mated[SWAP[j], k] = remote(it, 27 + 2 * SWAP[j] + k, part_out.at[it, j, k],
                                       part_in.at[it, SWAP[j], k], mate, z)
            if n >= 3:
                finish(*order[n - 3])
        for n in range(len(order) - 3, len(order)):
            finish(*order[n])
        return result

    image = apply(0, x_ref)
    for k in range(n_k):
        value = (diff[...] * x_ref[k].astype(F32) + 2.0 * image[k]) / half_width
        first_ref[k] = value
        second[k] = value.astype(BF16)
    image = apply(1, second)
    for k in range(n_k):
        filt_ref[k] = 2.0 * (diff[...] * second[k].astype(F32) + 2.0 * image[k]) / half_width - x_ref[k].astype(F32)
    for copy in sent:
        copy.wait_send()


def fused(n_pts, n_val, trials, psi_val, psi_cond, kernel, eps_val, eps_cond):
    n_k, rows, cols = trials.shape
    points = psi_val.shape[0]
    width = kernel.shape[1]
    vmem, hbm = pl.BlockSpec(memory_space=pltpu.VMEM), pl.BlockSpec(memory_space=pl.ANY)
    out = jax.ShapeDtypeStruct((n_k, rows, cols), F32)
    tile = (n_k, rows, cols)
    return pl.pallas_call(
        lambda *refs: fused_kernel(n_pts, n_val, *refs),
        out_shape=(out, out),
        in_specs=[vmem, hbm, hbm, hbm, vmem, vmem],
        out_specs=(vmem, vmem),
        scratch_shapes=[
            pltpu.VMEM((points, rows), BF16),
            pltpu.VMEM((rows, points), F32),
            pltpu.VMEM((4, points, 2 * cols), BF16),
            pltpu.VMEM(kernel.shape, BF16),
            pltpu.VMEM((rows, cols), F32),
            pltpu.VMEM(tile, BF16),
            pltpu.VMEM((2, 4, 2) + tile, BF16),
            pltpu.VMEM((2, n_val, n_k, width), F32),
            pltpu.VMEM((2, n_val, n_k, width), F32),
            pltpu.VMEM((2, n_pts, n_k, points), F32),
            pltpu.VMEM((2, n_pts, n_k, points), F32),
            pltpu.VMEM((2, n_k, points), F32),
            pltpu.VMEM((2, n_val, n_k, points), F32),
            pltpu.VMEM((4,) + tile, F32),
            pltpu.VMEM((2, 4) + tile, BF16),
            pltpu.VMEM((2, 4) + tile, BF16),
            pltpu.VMEM((2, 3) + tile, BF16),
            pltpu.VMEM((2, 3) + tile, BF16),
            pltpu.SemaphoreType.DMA((10,)),
            pltpu.SemaphoreType.DMA((2, 41)),
            pltpu.SemaphoreType.DMA((2, 41)),
        ],
        compiler_params=pltpu.CompilerParams(
            collective_id=0, has_side_effects=True, vmem_limit_bytes=60 * 1024 * 1024),
    )(trials, psi_val, psi_cond, kernel, eps_val.reshape(1, -1), eps_cond.reshape(1, -1))


def solution(mesh):
    n_pts, n_val = mesh.shape["pts"], mesh.shape["val"]

    def program(trials, *rest):
        whole_lanes = trials.shape[2] % 128 == 0 and rest[0].shape[1] % 128 == 0
        if whole_lanes and trials.shape[0] == 2 and n_pts == 8 and n_val <= 4:
            return fused(n_pts, n_val, trials, *rest)
        return local(trials, *rest)

    in_specs = (
        P(None, "val", "pts"),
        P("pts", "val"),
        P("pts", None),
        P(None, ("pts", "val")),
        P("val"),
        P(),
    )
    out_specs = (P(None, "val", "pts"), P(None, "val", "pts"))
    return jax.shard_map(program, mesh=mesh, in_specs=in_specs, out_specs=out_specs, check_vma=False)
```

```python
import jax
import jax.numpy as jnp
from jax import lax
from jax.experimental import pallas as pl
from jax.experimental.pallas import tpu as pltpu
from jax.sharding import PartitionSpec as P

center_shift = 1.75
half_width = 1.25


def gathered_inner(local_trial, psi_cond):
    return jnp.einsum(
        "kvc,mc->kvm",
        lax.all_gather(local_trial, "pts", axis=2, tiled=True),
        psi_cond,
        preferred_element_type=jnp.float32,
    )


def orbital_terms(inner, psi_val, psi_cond, kernel):
    rho_part = jnp.einsum("mv,kvm->km", psi_val.astype(jnp.float32), inner)
    rho = lax.psum_scatter(rho_part, "val", scatter_dimension=1, tiled=True).astype(jnp.bfloat16)
    image_part = jnp.einsum("km,nm->kn", rho, kernel, preferred_element_type=jnp.float32)
    image_rows = lax.psum_scatter(
        image_part.astype(jnp.bfloat16), "pts", scatter_dimension=1, tiled=True
    ).astype(jnp.float32)
    image = lax.psum(image_rows, "val")
    weighted = (jnp.transpose(psi_val.astype(jnp.float32))[None] * image[:, None, :]).astype(
        jnp.bfloat16
    )
    return jnp.einsum("kvm,mc->kvc", weighted, psi_cond, preferred_element_type=jnp.float32)


def reduced(partial_sum):
    return lax.psum_scatter(
        partial_sum.astype(jnp.bfloat16), "pts", scatter_dimension=2, tiled=True
    ).astype(jnp.float32)


def local(trials, psi_val, psi_cond, kernel, eps_val, eps_cond):
    cols_own = trials.shape[2]
    index_pts = lax.axis_index("pts")
    diff_whole = (eps_cond[None, :] - eps_val[:, None] - center_shift)[None]
    diff_own = lax.dynamic_slice_in_dim(diff_whole, index_pts * cols_own, cols_own, 2)
    first_image = reduced(
        orbital_terms(gathered_inner(trials, psi_cond), psi_val, psi_cond, kernel)
    )
    first = (diff_own * trials.astype(jnp.float32) + 2.0 * first_image) / half_width
    second_trial = first.astype(jnp.bfloat16)
    second_inner = gathered_inner(second_trial, psi_cond)
    second_image = reduced(orbital_terms(second_inner, psi_val, psi_cond, kernel))
    filtered = 2.0 * (
        diff_own * second_trial.astype(jnp.float32) + 2.0 * second_image
    ) / half_width - trials.astype(jnp.float32)
    return (first, filtered)


F32, BF16 = jnp.float32, jnp.bfloat16
SWAP = (0, 2, 1, 3)
NT = (((1,), (1,)), ((), ()))


def fused_kernel(n_pts, n_val, x_hbm, pv_hbm, pc_hbm, kern_hbm, ev_ref, ec_ref, first_ref, filt_ref,
                 x_ref, pv, pvt, cond, kern, diff, second, xg, rs, rr, im, ir, ws, wr,
                 acc, part_out, part_in, link_out, link_in, load_sem, send_sem, recv_sem):
    p = lax.axis_index("pts")
    z = lax.axis_index("val")
    core = lax.rem(p, 2)
    n_k, rows, cols = x_ref.shape
    pts_own = pv.shape[0]
    width = rr.shape[4]
    lanes = im.shape[4]

    def flipped(q, bit):
        return q + bit - 2 * bit * lax.rem(lax.div(q, bit), 2)

    bit_a, bit_b = 2 + 2 * core, 4 - 2 * core
    mate, nbr_a, nbr_b = flipped(p, 1), flipped(p, bit_a), flipped(p, bit_b)
    places = (p, nbr_a, nbr_b, flipped(nbr_a, bit_b))

    load_x = pltpu.make_async_copy(x_hbm, x_ref, load_sem.at[10])
    load_x.start()
    barrier = pltpu.get_barrier_semaphore()
    for r in range(1, n_pts):
        pl.semaphore_signal(barrier, inc=1, device_id=(lax.rem(p + r, n_pts), z), device_id_type=pl.DeviceIdType.MESH)
    for s in range(1, n_val):
        pl.semaphore_signal(barrier, inc=1, device_id=(p, lax.rem(z + s, n_val)), device_id_type=pl.DeviceIdType.MESH)
    loads = [pltpu.make_async_copy(pv_hbm, pv, load_sem.at[0])]
    for j in range(4):
        for h in range(2):
            owner = places[j] if h == 0 else flipped(places[j], 1)
            at = pl.multiple_of(owner * cols, cols)
            loads.append(pltpu.make_async_copy(
                pc_hbm.at[:, pl.ds(at, cols)], cond.at[j, :, pl.ds(h * cols, cols)], load_sem.at[1 + 2 * j + h]))
    loads.append(pltpu.make_async_copy(kern_hbm, kern, load_sem.at[9]))
    for load in loads:
        load.start()
    load_x.wait()
    pl.semaphore_wait(barrier, n_pts + n_val - 2)

    sent = []
    live = {}

    def remote(it, k, n, src, dst, to_p, to_z):
        copy = pltpu.make_async_remote_copy(
            src_ref=src, dst_ref=dst, send_sem=send_sem.at[it, k, n], recv_sem=recv_sem.at[it, k, n],
            device_id=(to_p, to_z), device_id_type=pl.DeviceIdType.MESH)
        copy.start()
        sent.append(copy)
        live[it, k, n] = copy

    def arrived(it, k, n):
        live[it, k, n].wait_recv()

    def gather_start(it, k, x):
        remote(it, k, 0, x.at[k], xg.at[it, 1, 0, k], nbr_a, z)
        remote(it, k, 1, x.at[k], xg.at[it, 2, 0, k], nbr_b, z)
        remote(it, k, 2, x.at[k], xg.at[it, 0, 1, k], mate, z)

    def gather_relay(it, k):
        arrived(it, k, 0)
        remote(it, k, 3, xg.at[it, 1, 0, k], xg.at[it, 3, 0, k], nbr_b, z)
        remote(it, k, 4, xg.at[it, 1, 0, k], xg.at[it, 2, 1, k], mate, z)
        arrived(it, k, 1)
        remote(it, k, 5, xg.at[it, 2, 0, k], xg.at[it, 1, 1, k], mate, z)

    def gather_last(it, k):
        arrived(it, k, 3)
        remote(it, k, 6, xg.at[it, 3, 0, k], xg.at[it, 3, 1, k], mate, z)

    def density(it, k, j, left, rho):
        step = 256
        arrived(it, k, (2, 5, 4, 6)[j])
        block = jnp.concatenate([left, xg[it, j, 1, k]], axis=1)
        out = []
        for t in range(pts_own // step):
            zz = lax.dot_general(block, cond[j, t * step:(t + 1) * step, :], NT, preferred_element_type=F32)
            y = zz * pvt[:, t * step:(t + 1) * step]
            out.append(jnp.sum(y.reshape(rows // 8, 8, step), axis=0))
        return out if rho is None else [u + w for u, w in zip(rho, out)]

    def rho_start(it, k, rho):
        row = jnp.concatenate([jnp.sum(u, axis=0, keepdims=True) for u in rho], axis=1)
        for s in range(n_val):
            rs[it, k, s] = row[:, s * width:(s + 1) * width]
        for s in range(1, n_val):
            to = lax.rem(z + s, n_val)
            remote(it, k, 6 + s, rs.at[it, k, to], rr.at[it, k, s], p, to)

    def tiled(row):
        return jnp.concatenate([row[:, i * lanes:(i + 1) * lanes] for i in range(pts_own // lanes)], axis=0)

    def image_start(it, k):
        own = rs[it, k, z]
        for s in range(1, n_val):
            arrived(it, k, 6 + s)
            own = own + rr[it, k, s]
        own = jnp.broadcast_to(own, (8, width)).astype(BF16)
        if it == 0 and k == 0:
            loads[9].wait()
        for t in range(n_pts):
            part = lax.dot_general(own, kern[t * pts_own:(t + 1) * pts_own, :], NT, preferred_element_type=F32)
            im[it, k, t] = tiled(part[:1])
        for r in range(1, n_pts):
            to = lax.rem(p + r, n_pts)
            remote(it, k, 9 + r, im.at[it, k, to], ir.at[it, k, r], to, z)

    def image_sum(it, k):
        total = im[it, k, p]
        for r in range(1, n_pts):
            arrived(it, k, 9 + r)
            total = total + ir[it, k, r]
        ws[it, k] = total
        for s in range(1, n_val):
            remote(it, k, 16 + s, ws.at[it, k], wr.at[it, k, s], p, lax.rem(z + s, n_val))

    def pairs_start(it, k):
        total = ws[it, k]
        for s in range(1, n_val):
            arrived(it, k, 16 + s)
            total = total + wr[it, k, s]
        row = jnp.concatenate([total[i:i + 1] for i in range(pts_own // lanes)], axis=1)
        weighted = (pvt[...] * row).astype(BF16)
        for j in (3, 2, 1, 0):
            both = jnp.dot(weighted, cond[j], preferred_element_type=F32)
            part_out[it, j, k] = both[:, cols:].astype(BF16)
            remote(it, k, 20 + SWAP[j], part_out.at[it, j, k], part_in.at[it, SWAP[j], k], mate, z)
            acc[j, k] = both[:, :cols]

    def chip_sum(it, k, j):
        arrived(it, k, 20 + j)
        return acc[j, k] + part_in[it, j, k].astype(F32)

    def pairs_send(it, k):
        link_out[it, 0, k] = chip_sum(it, k, 3).astype(BF16)
        remote(it, k, 24, link_out.at[it, 0, k], link_in.at[it, 0, k], nbr_b, z)
        link_out[it, 2, k] = chip_sum(it, k, 2).astype(BF16)
        remote(it, k, 25, link_out.at[it, 2, k], link_in.at[it, 2, k], nbr_b, z)

    def pairs_relay(it, k):
        value = chip_sum(it, k, 1)
        arrived(it, k, 24)
        link_out[it, 1, k] = (value + link_in[it, 0, k].astype(F32)).astype(BF16)
        remote(it, k, 26, link_out.at[it, 1, k], link_in.at[it, 1, k], nbr_a, z)

    def pairs_end(it, k):
        value = chip_sum(it, k, 0)
        arrived(it, k, 25)
        value = value + link_in[it, 2, k].astype(F32)
        arrived(it, k, 26)
        return value + link_in[it, 1, k].astype(F32)

    def apply(it, x, use):
        every = range(n_k)
        if it == 0:
            for k in every:
                gather_start(it, k, x)
            loads[0].wait()
            pvt[...] = jnp.transpose(pv[...].astype(F32))
            diff[...] = (ec_ref[:, pl.ds(pl.multiple_of(p * cols, cols), cols)]
                         - jnp.transpose(jnp.broadcast_to(ev_ref[...], (cols, rows))) - center_shift)
            for load in loads[1:9]:
                load.wait()
        rho = [None] * n_k
        for k in every:
            gather_relay(it, k)
            rho[k] = density(it, k, 0, x[k], None)
        for k in every:
            rho[k] = density(it, k, 1, xg[it, 1, 0, k], rho[k])
            gather_last(it, k)
            rho[k] = density(it, k, 2, xg[it, 2, 0, k], rho[k])
            rho[k] = density(it, k, 3, xg[it, 3, 0, k], rho[k])
            rho_start(it, k, rho[k])
        for stage in (image_start, image_sum):
            for k in every:
                stage(it, k)
        for k in every:
            pairs_start(it, k)
            pairs_send(it, k)
        for k in every:
            pairs_relay(it, k)
        for k in every:
            use(k, pairs_end(it, k))

    def to_first(k, image):
        value = (diff[...] * x_ref[k].astype(F32) + 2.0 * image) / half_width
        second[k] = value.astype(BF16)
        gather_start(1, k, second)
        first_ref[k] = value

    def to_filtered(k, image):
        filt_ref[k] = 2.0 * (diff[...] * second[k].astype(F32) + 2.0 * image) / half_width - x_ref[k].astype(F32)

    apply(0, x_ref, to_first)
    apply(1, second, to_filtered)
    for copy in sent:
        copy.wait_send()


def fused(n_pts, n_val, trials, psi_val, psi_cond, kernel, eps_val, eps_cond):
    n_k, rows, cols = trials.shape
    points = psi_val.shape[0]
    width = kernel.shape[1]
    vmem, hbm = pl.BlockSpec(memory_space=pltpu.VMEM), pl.BlockSpec(memory_space=pl.ANY)
    out = jax.ShapeDtypeStruct((n_k, rows, cols), F32)
    tile = (n_k, rows, cols)
    return pl.pallas_call(
        lambda *refs: fused_kernel(n_pts, n_val, *refs),
        out_shape=(out, out),
        in_specs=[hbm, hbm, hbm, hbm, vmem, vmem],
        out_specs=(vmem, vmem),
        scratch_shapes=[
            pltpu.VMEM(tile, BF16),
            pltpu.VMEM((points, rows), BF16),
            pltpu.VMEM((rows, points), F32),
            pltpu.VMEM((4, points, 2 * cols), BF16),
            pltpu.VMEM(kernel.shape, BF16),
            pltpu.VMEM((rows, cols), F32),
            pltpu.VMEM(tile, BF16),
            pltpu.VMEM((2, 4, 2) + tile, BF16),
            pltpu.VMEM((2, n_k, n_val, 1, width), F32),
            pltpu.VMEM((2, n_k, n_val, 1, width), F32),
            pltpu.VMEM((2, n_k, n_pts, points // 128, 128), F32),
            pltpu.VMEM((2, n_k, n_pts, points // 128, 128), F32),
            pltpu.VMEM((2, n_k, points // 128, 128), F32),
            pltpu.VMEM((2, n_k, n_val, points // 128, 128), F32),
            pltpu.VMEM((4,) + tile, F32),
            pltpu.VMEM((2, 4) + tile, BF16),
            pltpu.VMEM((2, 4) + tile, BF16),
            pltpu.VMEM((2, 3) + tile, BF16),
            pltpu.VMEM((2, 3) + tile, BF16),
            pltpu.SemaphoreType.DMA((11,)),
            pltpu.SemaphoreType.DMA((2, n_k, 27)),
            pltpu.SemaphoreType.DMA((2, n_k, 27)),
        ],
        compiler_params=pltpu.CompilerParams(
            collective_id=0, has_side_effects=True, vmem_limit_bytes=60 * 1024 * 1024),
    )(trials, psi_val, psi_cond, kernel, eps_val.reshape(1, -1), eps_cond.reshape(1, -1))


def solution(mesh):
    n_pts, n_val = mesh.shape["pts"], mesh.shape["val"]

    def program(trials, *rest):
        whole_lanes = trials.shape[2] % 128 == 0 and rest[0].shape[1] % 128 == 0
        if whole_lanes and trials.shape[0] == 2 and n_pts == 8 and n_val <= 4:
            return fused(n_pts, n_val, trials, *rest)
        return local(trials, *rest)

    in_specs = (
        P(None, "val", "pts"),
        P("pts", "val"),
        P("pts", None),
        P(None, ("pts", "val")),
        P("val"),
        P(),
    )
    out_specs = (P(None, "val", "pts"), P(None, "val", "pts"))
    return jax.shard_map(program, mesh=mesh, in_specs=in_specs, out_specs=out_specs, check_vma=False)
```

```python
import jax
import jax.numpy as jnp
from jax import lax
from jax.experimental import pallas as pl
from jax.experimental.pallas import tpu as pltpu
from jax.sharding import PartitionSpec as P

center_shift = 1.75
half_width = 1.25


def gathered_inner(local_trial, psi_cond):
    return jnp.einsum(
        "kvc,mc->kvm",
        lax.all_gather(local_trial, "pts", axis=2, tiled=True),
        psi_cond,
        preferred_element_type=jnp.float32,
    )


def orbital_terms(inner, psi_val, psi_cond, kernel):
    rho_part = jnp.einsum("mv,kvm->km", psi_val.astype(jnp.float32), inner)
    rho = lax.psum_scatter(rho_part, "val", scatter_dimension=1, tiled=True).astype(jnp.bfloat16)
    image_part = jnp.einsum("km,nm->kn", rho, kernel, preferred_element_type=jnp.float32)
    image_rows = lax.psum_scatter(
        image_part.astype(jnp.bfloat16), "pts", scatter_dimension=1, tiled=True
    ).astype(jnp.float32)
    image = lax.psum(image_rows, "val")
    weighted = (jnp.transpose(psi_val.astype(jnp.float32))[None] * image[:, None, :]).astype(
        jnp.bfloat16
    )
    return jnp.einsum("kvm,mc->kvc", weighted, psi_cond, preferred_element_type=jnp.float32)


def reduced(partial_sum):
    return lax.psum_scatter(
        partial_sum.astype(jnp.bfloat16), "pts", scatter_dimension=2, tiled=True
    ).astype(jnp.float32)


def local(trials, psi_val, psi_cond, kernel, eps_val, eps_cond):
    cols_own = trials.shape[2]
    index_pts = lax.axis_index("pts")
    diff_whole = (eps_cond[None, :] - eps_val[:, None] - center_shift)[None]
    diff_own = lax.dynamic_slice_in_dim(diff_whole, index_pts * cols_own, cols_own, 2)
    first_image = reduced(
        orbital_terms(gathered_inner(trials, psi_cond), psi_val, psi_cond, kernel)
    )
    first = (diff_own * trials.astype(jnp.float32) + 2.0 * first_image) / half_width
    second_trial = first.astype(jnp.bfloat16)
    second_inner = gathered_inner(second_trial, psi_cond)
    second_image = reduced(orbital_terms(second_inner, psi_val, psi_cond, kernel))
    filtered = 2.0 * (
        diff_own * second_trial.astype(jnp.float32) + 2.0 * second_image
    ) / half_width - trials.astype(jnp.float32)
    return (first, filtered)


F32, BF16 = jnp.float32, jnp.bfloat16
SWAP = (0, 2, 1, 3)
NT = (((1,), (1,)), ((), ()))


def fused_kernel(n_pts, n_val, x_hbm, pv_hbm, pc_hbm, kern_hbm, ev_ref, ec_ref, first_ref, filt_ref,
                 x_ref, pv, pvt, cond, kern, diff, second, xg, rs, rr, im, ir, ws, wr,
                 acc, part_out, part_in, link_out, link_in, load_sem, send_sem, recv_sem):
    p = lax.axis_index("pts")
    z = lax.axis_index("val")
    core = lax.rem(p, 2)
    n_k, rows, cols = x_ref.shape
    pts_own = pv.shape[0]
    width = rr.shape[4]
    lanes = im.shape[4]

    def flipped(q, bit):
        return q + bit - 2 * bit * lax.rem(lax.div(q, bit), 2)

    bit_a, bit_b = 2 + 2 * core, 4 - 2 * core
    mate, nbr_a, nbr_b = flipped(p, 1), flipped(p, bit_a), flipped(p, bit_b)
    places = (p, nbr_a, nbr_b, flipped(nbr_a, bit_b))

    load_x = pltpu.make_async_copy(x_hbm, x_ref, load_sem.at[10])
    load_x.start()
    barrier = pltpu.get_barrier_semaphore()
    for r in range(1, n_pts):
        pl.semaphore_signal(barrier, inc=1, device_id=(lax.rem(p + r, n_pts), z), device_id_type=pl.DeviceIdType.MESH)
    for s in range(1, n_val):
        pl.semaphore_signal(barrier, inc=1, device_id=(p, lax.rem(z + s, n_val)), device_id_type=pl.DeviceIdType.MESH)
    loads = [pltpu.make_async_copy(pv_hbm, pv, load_sem.at[0])]
    for j in range(4):
        for h in range(2):
            owner = places[j] if h == 0 else flipped(places[j], 1)
            at = pl.multiple_of(owner * cols, cols)
            loads.append(pltpu.make_async_copy(
                pc_hbm.at[:, pl.ds(at, cols)], cond.at[j, :, pl.ds(h * cols, cols)], load_sem.at[1 + 2 * j + h]))
    loads.append(pltpu.make_async_copy(kern_hbm, kern, load_sem.at[9]))
    for load in loads:
        load.start()
    load_x.wait()
    pl.semaphore_wait(barrier, n_pts + n_val - 2)

    sent = []
    live = {}

    def remote(it, k, n, src, dst, to_p, to_z):
        copy = pltpu.make_async_remote_copy(
            src_ref=src, dst_ref=dst, send_sem=send_sem.at[it, k, n], recv_sem=recv_sem.at[it, k, n],
            device_id=(to_p, to_z), device_id_type=pl.DeviceIdType.MESH)
        copy.start()
        sent.append(copy)
        live[it, k, n] = copy

    def arrived(it, k, n):
        live[it, k, n].wait_recv()

    def gather_start(it, k, x):
        remote(it, k, 0, x.at[k], xg.at[it, 1, 0, k], nbr_a, z)
        remote(it, k, 1, x.at[k], xg.at[it, 2, 0, k], nbr_b, z)
        remote(it, k, 2, x.at[k], xg.at[it, 0, 1, k], mate, z)

    def gather_relay(it, k):
        arrived(it, k, 0)
        remote(it, k, 3, xg.at[it, 1, 0, k], xg.at[it, 3, 0, k], nbr_b, z)
        remote(it, k, 4, xg.at[it, 1, 0, k], xg.at[it, 2, 1, k], mate, z)
        arrived(it, k, 1)
        remote(it, k, 5, xg.at[it, 2, 0, k], xg.at[it, 1, 1, k], mate, z)

    def gather_last(it, k):
        arrived(it, k, 3)
        remote(it, k, 6, xg.at[it, 3, 0, k], xg.at[it, 3, 1, k], mate, z)

    def density(it, k, j, left, rho):
        step = 256
        arrived(it, k, (2, 5, 4, 6)[j])
        block = jnp.concatenate([left, xg[it, j, 1, k]], axis=1)
        out = []
        for t in range(pts_own // step):
            zz = lax.dot_general(block, cond[j, t * step:(t + 1) * step, :], NT, preferred_element_type=F32)
            y = zz * pvt[:, t * step:(t + 1) * step]
            out.append(jnp.sum(y.reshape(rows // 8, 8, step), axis=0))
        return out if rho is None else [u + w for u, w in zip(rho, out)]

    def rho_start(it, k, rho):
        row = jnp.concatenate([jnp.sum(u, axis=0, keepdims=True) for u in rho], axis=1)
        for s in range(n_val):
            rs[it, k, s] = row[:, s * width:(s + 1) * width]
        for s in range(1, n_val):
            to = lax.rem(z + s, n_val)
            remote(it, k, 6 + s, rs.at[it, k, to], rr.at[it, k, s], p, to)

    def tiled(row):
        return jnp.concatenate([row[:, i * lanes:(i + 1) * lanes] for i in range(pts_own // lanes)], axis=0)

    def image_start(it, k):
        own = rs[it, k, z]
        for s in range(1, n_val):
            arrived(it, k, 6 + s)
            own = own + rr[it, k, s]
        own = jnp.broadcast_to(own, (8, width)).astype(BF16)
        if it == 0 and k == 0:
            loads[9].wait()
        for t in range(n_pts):
            part = lax.dot_general(own, kern[t * pts_own:(t + 1) * pts_own, :], NT, preferred_element_type=F32)
            im[it, k, t] = tiled(part[:1])
        for r in range(1, n_pts):
            to = lax.rem(p + r, n_pts)
            remote(it, k, 9 + r, im.at[it, k, to], ir.at[it, k, r], to, z)

    def image_sum(it, k):
        total = im[it, k, p]
        for r in range(1, n_pts):
            arrived(it, k, 9 + r)
            total = total + ir[it, k, r]
        ws[it, k] = total
        for s in range(1, n_val):
            remote(it, k, 16 + s, ws.at[it, k], wr.at[it, k, s], p, lax.rem(z + s, n_val))

    def pairs_start(it, k):
        total = ws[it, k]
        for s in range(1, n_val):
            arrived(it, k, 16 + s)
            total = total + wr[it, k, s]
        row = jnp.concatenate([total[i:i + 1] for i in range(pts_own // lanes)], axis=1)
        weighted = (pvt[...] * row).astype(BF16)
        for j in (3, 2, 1, 0):
            both = jnp.dot(weighted, cond[j], preferred_element_type=F32)
            part_out[it, j, k] = both[:, cols:].astype(BF16)
            remote(it, k, 20 + SWAP[j], part_out.at[it, j, k], part_in.at[it, SWAP[j], k], mate, z)
            acc[j, k] = both[:, :cols]
            if j == 1:
                pairs_send(it, k, 3, 0, 24)
            elif j == 0:
                pairs_send(it, k, 2, 2, 25)

    def chip_sum(it, k, j):
        arrived(it, k, 20 + j)
        return acc[j, k] + part_in[it, j, k].astype(F32)

    def pairs_send(it, k, j, slot, n):
        link_out[it, slot, k] = chip_sum(it, k, j).astype(BF16)
        remote(it, k, n, link_out.at[it, slot, k], link_in.at[it, slot, k], nbr_b, z)

    def pairs_relay(it, k):
        value = chip_sum(it, k, 1)
        arrived(it, k, 24)
        link_out[it, 1, k] = (value + link_in[it, 0, k].astype(F32)).astype(BF16)
        remote(it, k, 26, link_out.at[it, 1, k], link_in.at[it, 1, k], nbr_a, z)

    def pairs_end(it, k):
        value = chip_sum(it, k, 0)
        arrived(it, k, 25)
        value = value + link_in[it, 2, k].astype(F32)
        arrived(it, k, 26)
        return value + link_in[it, 1, k].astype(F32)

    def apply(it, x, use):
        every = range(n_k)
        if it == 0:
            for k in every:
                gather_start(it, k, x)
            loads[0].wait()
            pvt[...] = jnp.transpose(pv[...].astype(F32))
            diff[...] = (ec_ref[:, pl.ds(pl.multiple_of(p * cols, cols), cols)]
                         - jnp.transpose(jnp.broadcast_to(ev_ref[...], (cols, rows))) - center_shift)
            for load in loads[1:9]:
                load.wait()
        rho = [None] * n_k
        for k in every:
            gather_relay(it, k)
            rho[k] = density(it, k, 0, x[k], None)
        for k in every:
            rho[k] = density(it, k, 1, xg[it, 1, 0, k], rho[k])
            gather_last(it, k)
            rho[k] = density(it, k, 2, xg[it, 2, 0, k], rho[k])
            rho[k] = density(it, k, 3, xg[it, 3, 0, k], rho[k])
            rho_start(it, k, rho[k])
        for stage in (image_start, image_sum):
            for k in every:
                stage(it, k)
        for k in every:
            pairs_start(it, k)
        for k in every:
            pairs_relay(it, k)
        for k in every:
            use(k, pairs_end(it, k))

    def to_first(k, image):
        value = (diff[...] * x_ref[k].astype(F32) + 2.0 * image) / half_width
        second[k] = value.astype(BF16)
        gather_start(1, k, second)
        first_ref[k] = value

    def to_filtered(k, image):
        filt_ref[k] = 2.0 * (diff[...] * second[k].astype(F32) + 2.0 * image) / half_width - x_ref[k].astype(F32)

    apply(0, x_ref, to_first)
    apply(1, second, to_filtered)
    for copy in sent:
        copy.wait_send()


def fused(n_pts, n_val, trials, psi_val, psi_cond, kernel, eps_val, eps_cond):
    n_k, rows, cols = trials.shape
    points = psi_val.shape[0]
    width = kernel.shape[1]
    vmem, hbm = pl.BlockSpec(memory_space=pltpu.VMEM), pl.BlockSpec(memory_space=pl.ANY)
    out = jax.ShapeDtypeStruct((n_k, rows, cols), F32)
    tile = (n_k, rows, cols)
    return pl.pallas_call(
        lambda *refs: fused_kernel(n_pts, n_val, *refs),
        out_shape=(out, out),
        in_specs=[hbm, hbm, hbm, hbm, vmem, vmem],
        out_specs=(vmem, vmem),
        scratch_shapes=[
            pltpu.VMEM(tile, BF16),
            pltpu.VMEM((points, rows), BF16),
            pltpu.VMEM((rows, points), F32),
            pltpu.VMEM((4, points, 2 * cols), BF16),
            pltpu.VMEM(kernel.shape, BF16),
            pltpu.VMEM((rows, cols), F32),
            pltpu.VMEM(tile, BF16),
            pltpu.VMEM((2, 4, 2) + tile, BF16),
            pltpu.VMEM((2, n_k, n_val, 1, width), F32),
            pltpu.VMEM((2, n_k, n_val, 1, width), F32),
            pltpu.VMEM((2, n_k, n_pts, points // 128, 128), F32),
            pltpu.VMEM((2, n_k, n_pts, points // 128, 128), F32),
            pltpu.VMEM((2, n_k, points // 128, 128), F32),
            pltpu.VMEM((2, n_k, n_val, points // 128, 128), F32),
            pltpu.VMEM((4,) + tile, F32),
            pltpu.VMEM((2, 4) + tile, BF16),
            pltpu.VMEM((2, 4) + tile, BF16),
            pltpu.VMEM((2, 3) + tile, BF16),
            pltpu.VMEM((2, 3) + tile, BF16),
            pltpu.SemaphoreType.DMA((11,)),
            pltpu.SemaphoreType.DMA((2, n_k, 27)),
            pltpu.SemaphoreType.DMA((2, n_k, 27)),
        ],
        compiler_params=pltpu.CompilerParams(
            collective_id=0, has_side_effects=True, vmem_limit_bytes=60 * 1024 * 1024),
    )(trials, psi_val, psi_cond, kernel, eps_val.reshape(1, -1), eps_cond.reshape(1, -1))


def solution(mesh):
    n_pts, n_val = mesh.shape["pts"], mesh.shape["val"]

    def program(trials, *rest):
        whole_lanes = trials.shape[2] % 128 == 0 and rest[0].shape[1] % 128 == 0
        if whole_lanes and trials.shape[0] == 2 and n_pts == 8 and n_val <= 4:
            return fused(n_pts, n_val, trials, *rest)
        return local(trials, *rest)

    in_specs = (
        P(None, "val", "pts"),
        P("pts", "val"),
        P("pts", None),
        P(None, ("pts", "val")),
        P("val"),
        P(),
    )
    out_specs = (P(None, "val", "pts"), P(None, "val", "pts"))
    return jax.shard_map(program, mesh=mesh, in_specs=in_specs, out_specs=out_specs, check_vma=False)
```
